32 devices in a mesh: parts: 2 (over y), row: 4 (over x, core), col: 4 (over z).
Axes of the slice: x: 2, y: 2, z: 4, core: 2. Of those that a mesh axis runs over, the one named last changes fastest.
Arguments:
- alignment_tensor: bfloat16 [256, 256, 256], P(('parts', 'col'), 'row'), parts along dimension 0, may hold values from -6 to 6
- standardizer_scaling: float32 [256], replicated, may hold values from 0.25 to 1.75
- standardizer_offset: float32 [256], replicated, may hold values from -3 to 3
- first_projector: bfloat16 [256, 32], replicated, may hold values from -0.375 to 0.375
- second_projector: bfloat16 [256, 32], replicated, may hold values from -0.375 to 0.375
- final_projector: bfloat16 [1024, 128], replicated, may hold values from -1 to 1
- final_offset: float32 [128], replicated, may hold values from -3 to 3
- amino_strand_label: int32 [512], P('parts'), parts along dimension 0, may hold values from 0 to 7, never falling along the last dimension, each value on 1 to 128 neighbouring positions
- matched_strand_count: int32 [16, 8], P('parts'), parts along dimension 0, may hold values from 32 to 128, as said below
- couple_delta_adjoint: bfloat16 [512, 256, 128], P(('parts', 'row'), 'col'), parts along dimension 0, may hold values from -6 to 6
Outputs:
- pair_update: bfloat16 [512, 256, 128], P(('parts', 'row'), 'col'), parts along dimension 0
- adjoint_first_factor: bfloat16 [256, 8192], P(('parts', 'col'), 'row'), parts along dimension 0
- grad_right: bfloat16 [256, 8192], P(('parts', 'col'), 'row'), parts along dimension 0
- grad_w_out: float32 [2048, 128], P('parts'), parts along dimension 0
The draws below stay inside these ranges and needn't reach their ends.
There are 2 independent parts, one for each index of `parts`. The reference program is written for one: setup_inputs(seed, part) draws one part's arguments, and reference() takes and returns one part's arrays. A program takes and returns all parts, laid end to end along the dimension named above; an argument that names none is the same for every part. Nothing has to cross between parts.
Inputs may be any that keep to these rules, and one draw needn't show every extreme that they name: `amino_strand_label`: chain numbers never fall along the residues; a chain has 1 to 128 residues. `matched_strand_count`: every entry is a multiple of 32.
All inputs are finite; a program needn't handle non-finite values.
Results may differ from the reference program's by a relative error of at most 0.018.
Values may be sent and summed in bfloat16 or wider, within the bound.
A program may use at most 256 MiB of HBM per device.

```python
import math
import jax
import jax.numpy as jnp
import numpy as np
from jax import lax

ALIGNED_HOMOLOGS = 128
ALIGNED_FEATS = 256
PROJECTED_SIZE = 32
CZ = 128
WINDOW_AMINOS = 256
DEPTH_STEP = 32
CHAINS = 8
LEVELS = 4
N_ROW = 4


def draw_matched_strand_count(key, part):
    levels = jax.random.randint(jax.random.fold_in(key, 11), (CHAINS * CHAINS,), 1, LEVELS + 1)
    spots = jax.random.permutation(jax.random.fold_in(key, 12), CHAINS * CHAINS)
    levels = levels.at[spots[0]].set(LEVELS).at[spots[1]].set(1)
    return (levels * DEPTH_STEP).reshape(CHAINS, CHAINS).astype(jnp.int32)


def steps_of(key, shape, shards, smallest, top_value):
    def one(dim, shards_of):
        steps = jax.random.uniform(jax.random.fold_in(jax.random.fold_in(key, 6), dim), (shards_of,), jnp.float32, smallest / len(shards), top_value / len(shards))
        return jnp.repeat(jnp.exp(steps), shape[dim] // shards_of).reshape((-1,) + (1,) * (len(shape) - dim - 1))

    loudness = one(*shards[0])
    for cut in shards[1:]:
        loudness = loudness * one(*cut)
    return loudness


def length_profile(amount, total, reach, lean):
    weights = [(1 << 20) // math.isqrt(grade ** lean) + 1 for grade in range(2, amount + 1)]
    rest, counts = total - reach - (amount - 1), [1] * (amount - 1)
    while rest > 0:
        free = [i for i in range(amount - 1) if counts[i] < reach]
        pool, budget = sum([weights[i] for i in free]), rest
        for i in free:
            more = min(reach - counts[i], max(1, budget * weights[i] // pool), rest)
            counts[i] = counts[i] + more
            rest = rest - more
    return np.array([reach] + counts)


def uneven(stream_key, amount, total, bound, slope):
    if amount == 2:
        one = jax.random.randint(stream_key, (), max(1, total - bound), min(bound, total - 1) + 1)
        return jnp.stack([one, total - one])
    sizes = jnp.asarray(length_profile(amount, total, bound, slope), jnp.int32)
    twos = (amount - 1) // 2
    donor, taker = sizes[1:1 + 2 * twos:2], sizes[2:2 + 2 * twos:2]
    slack = jnp.minimum(donor - 1, bound - taker)
    shifted = jax.random.randint(jax.random.fold_in(stream_key, 1), (twos,), 0, 1 << 20) % (slack + 1)
    sizes = sizes.at[1:1 + 2 * twos:2].set(donor - shifted).at[2:2 + 2 * twos:2].set(taker + shifted)
    return sizes[jax.random.permutation(jax.random.fold_in(stream_key, 2), amount)]


def bell_draw(own_key, shape, scale, limit, cuts=(), held_as=jnp.bfloat16):
    array = scale * jax.random.normal(own_key, shape, jnp.float32)
    if cuts:
        array = array * steps_of(own_key, shape, cuts, -0.22, 0.18)
    return jnp.clip(array, -limit, limit).astype(held_as)


def setup_inputs(seed: int = 0, part: int = 0) -> dict:
    key_of = jax.random.split(jax.random.key(seed), 11)
    part_splits = jax.random.split(jax.random.fold_in(key_of[10], part), 11)
    return {
        "alignment_tensor": bell_draw(part_splits[0], (ALIGNED_HOMOLOGS, WINDOW_AMINOS, ALIGNED_FEATS), 1.0, 6.0, ((0, 4), (1, 4))),
        "standardizer_scaling": jnp.clip(1.0 + 0.15 * jax.random.normal(key_of[1], (ALIGNED_FEATS,), jnp.float32), 0.25, 1.75),
        "standardizer_offset": bell_draw(key_of[2], (ALIGNED_FEATS,), 0.5, 3.0, (), jnp.float32),
        "first_projector": bell_draw(key_of[3], (ALIGNED_FEATS, PROJECTED_SIZE), ALIGNED_FEATS ** -0.5, 0.375),
        "second_projector": bell_draw(key_of[4], (ALIGNED_FEATS, PROJECTED_SIZE), ALIGNED_FEATS ** -0.5, 0.375),
        "final_projector": bell_draw(key_of[5], (PROJECTED_SIZE * PROJECTED_SIZE, CZ), PROJECTED_SIZE ** -0.5, 1.0),
        "final_offset": bell_draw(key_of[6], (CZ,), 0.5, 3.0, (), jnp.float32),
        "amino_strand_label": jnp.searchsorted(jnp.cumsum(uneven(part_splits[7], CHAINS, WINDOW_AMINOS, WINDOW_AMINOS // 2, 1)), jnp.arange(WINDOW_AMINOS), side="right").astype(jnp.int32),
        "matched_strand_count": draw_matched_strand_count(jax.random.fold_in(jax.random.fold_in(key_of[10], part), 71), part),
        "couple_delta_adjoint": bell_draw(part_splits[9], (WINDOW_AMINOS, WINDOW_AMINOS, CZ), 1.0, 6.0, ((0, 4), (1, 4))),
    }


def standardize_entries(alignment_tensor, standard_multiplier, additive_offset):
    incoming_entries = alignment_tensor.astype(jnp.float32)
    center = incoming_entries - lax.optimization_barrier(jnp.mean(incoming_entries, axis=-1, keepdims=True))
    spread = lax.optimization_barrier(jnp.mean(center * center, axis=-1, keepdims=True))
    return (center * lax.rsqrt(spread + 1e-05) * standard_multiplier + additive_offset).astype(jnp.bfloat16)

def reference(alignment_tensor, standardizer_scaling, standardizer_offset, first_projector, second_projector, final_projector, final_offset, amino_strand_label, matched_strand_count, couple_delta_adjoint):
    standardized_entries = standardize_entries(alignment_tensor, standardizer_scaling, standardizer_offset).reshape(-1, ALIGNED_FEATS)
    first_factor = jnp.dot(standardized_entries, first_projector, preferred_element_type=jnp.float32).astype(jnp.bfloat16).reshape(ALIGNED_HOMOLOGS, WINDOW_AMINOS * PROJECTED_SIZE)
    second_factor = jnp.dot(standardized_entries, second_projector, preferred_element_type=jnp.float32).astype(jnp.bfloat16).reshape(ALIGNED_HOMOLOGS, WINDOW_AMINOS * PROJECTED_SIZE)
    chains = jnp.arange(CHAINS, dtype=jnp.int32)
    onehot = (amino_strand_label[:, None] == chains[None, :]).astype(jnp.float32)
    table = matched_strand_count.astype(jnp.float32)
    depth = jnp.dot(jnp.dot(onehot, table, precision=lax.Precision.HIGHEST), onehot.T, precision=lax.Precision.HIGHEST)
    block = WINDOW_AMINOS // N_ROW
    right_wide = second_factor.astype(jnp.float32)

    def row_block(index):
        start = (index * block).astype(jnp.int32)
        left_rows = lax.dynamic_slice_in_dim(first_factor, start * PROJECTED_SIZE, block * PROJECTED_SIZE, 1).astype(jnp.float32)
        depth_rows = lax.dynamic_slice_in_dim(depth, start, block, 0)
        grad_rows = lax.dynamic_slice_in_dim(couple_delta_adjoint, start, block, 0)
        acc = jnp.zeros((block, WINDOW_AMINOS, PROJECTED_SIZE * PROJECTED_SIZE), jnp.float32)
        for level in range(LEVELS):
            low = level * DEPTH_STEP
            prod = jnp.einsum('sa,sb->ab', left_rows[low:low + DEPTH_STEP], right_wide[low:low + DEPTH_STEP])
            prod = prod.reshape(block, PROJECTED_SIZE, WINDOW_AMINOS, PROJECTED_SIZE).transpose(0, 2, 1, 3).reshape(block, WINDOW_AMINOS, PROJECTED_SIZE * PROJECTED_SIZE)
            acc = acc + (depth_rows > low).astype(jnp.float32)[:, :, None] * prod
        outer = (acc / depth_rows[:, :, None]).astype(jnp.bfloat16)
        flat_outer = outer.reshape(-1, PROJECTED_SIZE * PROJECTED_SIZE)
        pair = (jnp.dot(flat_outer, final_projector, preferred_element_type=jnp.float32) + final_offset).astype(jnp.bfloat16)
        flat_grad = grad_rows.reshape(-1, CZ)
        back = jnp.dot(flat_grad, final_projector.T, preferred_element_type=jnp.float32).reshape(block, WINDOW_AMINOS, PROJECTED_SIZE * PROJECTED_SIZE)
        scaled = (back / depth_rows[:, :, None]).astype(jnp.bfloat16)
        weight_part = jnp.dot(flat_outer.T, flat_grad, preferred_element_type=jnp.float32)
        turned = scaled.reshape(block, WINDOW_AMINOS, PROJECTED_SIZE, PROJECTED_SIZE).transpose(0, 2, 1, 3).reshape(block * PROJECTED_SIZE, WINDOW_AMINOS * PROJECTED_SIZE).astype(jnp.float32)
        left_parts = []
        right_parts = []
        for level in range(LEVELS):
            low = level * DEPTH_STEP
            keep = (depth_rows > low).astype(jnp.float32)
            keep_wide = jnp.broadcast_to(keep[:, None, :, None], (block, PROJECTED_SIZE, WINDOW_AMINOS, PROJECTED_SIZE)).reshape(block * PROJECTED_SIZE, WINDOW_AMINOS * PROJECTED_SIZE)
            masked = turned * keep_wide
            left_parts.append(jnp.einsum('sb,ab->sa', right_wide[low:low + DEPTH_STEP], masked))
            right_parts.append(jnp.einsum('sa,ab->sb', left_rows[low:low + DEPTH_STEP], masked))
        return (pair.reshape(block, WINDOW_AMINOS, CZ), jnp.concatenate(left_parts, 0), jnp.concatenate(right_parts, 0), weight_part)
    pairs, first_factor_adjoint, right_grads, weight_parts = lax.map(row_block, jnp.arange(N_ROW, dtype=jnp.int32))
    pair_update = pairs.reshape(WINDOW_AMINOS, WINDOW_AMINOS, CZ)
    adjoint_first_factor = first_factor_adjoint.transpose(1, 0, 2).reshape(ALIGNED_HOMOLOGS, WINDOW_AMINOS * PROJECTED_SIZE).astype(jnp.bfloat16)
    grad_right = lax.optimization_barrier(jnp.sum(right_grads, axis=0)).astype(jnp.bfloat16)
    grad_w_out = lax.optimization_barrier(jnp.sum(weight_parts, axis=0)) / WINDOW_AMINOS
    return (pair_update, adjoint_first_factor, grad_right, grad_w_out)
```

```python
import functools

import jax
import jax.numpy as jnp
from jax import lax
from jax.experimental import pallas as pl
from jax.experimental.pallas import tpu as pltpu
from jax.sharding import PartitionSpec as P

PROJECTED_SIZE = 32
CZ = 128
WINDOW_AMINOS = 256
DEPTH_STEP = 32
CHAINS = 8
LEVELS = 4


def standardize_entries(alignment_tensor, standard_multiplier, additive_offset):
    incoming_entries = alignment_tensor.astype(jnp.float32)
    center = incoming_entries - jnp.mean(incoming_entries, axis=-1, keepdims=True)
    spread = jnp.mean(center * center, axis=-1, keepdims=True)
    return (center * lax.rsqrt(spread + 1e-05) * standard_multiplier + additive_offset).astype(
        jnp.bfloat16
    )


def pair_kernel(
    group, cols, seqs, levels,
    left_ref, right_ref, depth_ref, grad_ref, weight_ref, weight_t_ref, bias_ref, left_t_ref,
    tall_ref,
    pair_ref, left_grad_ref, right_grad_ref, weight_grad_ref,
    outer_ref, scaled_ref, back_ref,
):
    step = pl.program_id(0)
    width = group * cols
    size = PROJECTED_SIZE
    chunk = 4
    depth = depth_ref[0]
    inverse = 1.0 / depth
    row = lax.broadcasted_iota(jnp.int32, (group * seqs, width), 0)
    lane = lax.broadcasted_iota(jnp.int32, (group * seqs, width), 1)
    seq = (row % seqs).astype(jnp.float32)
    keep = jnp.where(
        jnp.logical_and(row // seqs == lane // cols, seq < depth), 1.0, 0.0
    ).astype(jnp.bfloat16)
    keep = jnp.concatenate([keep] * chunk, axis=1)
    grad = grad_ref[...]
    back = lax.dot_general(
        weight_ref[...], grad, (((1,), (1,)), ((), ())), preferred_element_type=jnp.float32
    )
    back_ref[...] = (back * inverse).astype(jnp.bfloat16)
    left = left_ref[0]
    left_grad = jnp.zeros((size, group * seqs), jnp.float32)
    rows_here = pl.ds(pl.multiple_of(step * size, size), size)
    for first in range(0, size, chunk):
        lanes = slice(first * width, (first + chunk) * width)
        right = right_ref[:, lanes] * keep
        prod = jnp.dot(left, right, preferred_element_type=jnp.float32)
        for e in range(chunk):
            outer_ref[(first + e) * size : (first + e + 1) * size, :] = (
                prod[:, e * width : (e + 1) * width] * inverse
            ).astype(jnp.bfloat16)
        scaled = jnp.concatenate(
            [back_ref[(first + e) * size : (first + e + 1) * size, :] for e in range(chunk)], axis=1
        )
        scaled_ref[rows_here, lanes] = scaled
        left_grad = left_grad + lax.dot_general(
            scaled, right, (((1,), (1,)), ((), ())), preferred_element_type=jnp.float32
        )
    left_grad_ref[0] = left_grad.astype(jnp.bfloat16)
    outer = outer_ref[...]
    pair = jnp.dot(weight_t_ref[...], outer, preferred_element_type=jnp.float32).T
    pair_ref[...] = (pair + bias_ref[...]).astype(jnp.bfloat16)
    weight_part = jnp.dot(outer, grad, preferred_element_type=jnp.float32)

    @pl.when(step == 0)
    def _():
        weight_grad_ref[...] = weight_part

    @pl.when(step > 0)
    def _():
        weight_grad_ref[...] += weight_part

    @pl.when(step == pl.num_programs(0) - 1)
    def _():
        span = 2
        part = lax.broadcasted_iota(jnp.int32, (DEPTH_STEP, span * width), 1) % width // cols
        for level in range(levels):
            wanted = jnp.where(tall_ref[...] > level * DEPTH_STEP, 1.0, 0.0).astype(jnp.bfloat16)
            wanted = jnp.concatenate([wanted] * span, axis=1)

            def piece(index, carry, level=level, wanted=wanted):
                lanes = pl.ds(pl.multiple_of(index * span * width, span * width), span * width)
                masked = scaled_ref[:, lanes] * wanted
                out = jnp.dot(left_t_ref[level], masked, preferred_element_type=jnp.float32)
                total = jnp.zeros((DEPTH_STEP, span * width), jnp.float32)
                for g in range(group):
                    total = jnp.where(part == g, out[g * DEPTH_STEP : (g + 1) * DEPTH_STEP], total)
                right_grad_ref[level * DEPTH_STEP : (level + 1) * DEPTH_STEP, lanes] = total
                return carry

            lax.fori_loop(0, size // span, piece, 0)


def shards(
    alignment_tensor,
    standardizer_scaling,
    standardizer_offset,
    first_projector,
    second_projector,
    final_projector,
    final_offset,
    amino_strand_label,
    matched_strand_count,
    couple_delta_adjoint,
):
    homolog_portion, rows, embedding_extent = alignment_tensor.shape
    cols = couple_delta_adjoint.shape[1]
    size = PROJECTED_SIZE
    entries = standardize_entries(
        alignment_tensor, standardizer_scaling, standardizer_offset
    ).reshape(-1, embedding_extent)
    both = jnp.dot(
        entries,
        jnp.concatenate([first_projector, second_projector], axis=1),
        preferred_element_type=jnp.float32,
    ).astype(jnp.bfloat16)
    first_factor = both[:, :size].reshape(homolog_portion, rows * size)
    second_factor = both[:, size:].reshape(homolog_portion, rows * size)
    left_panel = lax.all_gather(first_factor, "col", axis=0, tiled=True)
    right_rows = lax.all_gather(second_factor, "row", axis=1, tiled=True)
    right_panel = lax.all_to_all(right_rows, "col", split_axis=1, concat_axis=0, tiled=True)
    seqs = left_panel.shape[0]
    levels = seqs // DEPTH_STEP
    row_start = lax.axis_index("row") * rows
    col_start = lax.axis_index("col") * cols
    chains = jnp.arange(CHAINS, dtype=jnp.int32)
    row_hot = (
        lax.dynamic_slice_in_dim(amino_strand_label, row_start, rows, 0)[:, None] == chains[None, :]
    ).astype(jnp.float32)
    col_hot = (
        lax.dynamic_slice_in_dim(amino_strand_label, col_start, cols, 0)[:, None] == chains[None, :]
    ).astype(jnp.float32)
    table = matched_strand_count.astype(jnp.float32)
    depth = jnp.dot(
        jnp.dot(row_hot, table, precision=lax.Precision.HIGHEST),
        col_hot.T,
        precision=lax.Precision.HIGHEST,
    )
    group = max(1, 128 // cols)
    width = group * cols
    steps = rows // group
    left4 = left_panel.reshape(seqs, steps, group, size)
    left_groups = left4.transpose(1, 3, 2, 0).reshape(steps, size, group * seqs)
    left_levels = (
        left_panel.reshape(levels, DEPTH_STEP, steps, group, size)
        .transpose(0, 3, 1, 2, 4)
        .reshape(levels, group * DEPTH_STEP, steps * size)
    )
    right_turned = right_panel.reshape(seqs, cols, size).transpose(0, 2, 1)
    right_wide = jnp.broadcast_to(
        right_turned[None, :, :, None, :], (group, seqs, size, group, cols)
    ).reshape(group * seqs, size * width)
    depth_rows = depth.reshape(steps, 1, width)
    depth_tall = jnp.broadcast_to(depth_rows, (steps, size, width)).reshape(steps * size, width)
    weight = final_projector.reshape(size, size, CZ).transpose(1, 0, 2).reshape(size * size, CZ)
    flat_grad = couple_delta_adjoint.reshape(-1, CZ)
    whole = lambda shape: pl.BlockSpec(shape, lambda g: (0,) * len(shape))
    pair, left_grad, right_grad, weight_part = pl.pallas_call(
        functools.partial(pair_kernel, group, cols, seqs, levels),
        grid=(steps,),
        in_specs=[
            pl.BlockSpec((1, size, group * seqs), lambda g: (g, 0, 0)),
            whole((group * seqs, size * width)),
            pl.BlockSpec((1, 1, width), lambda g: (g, 0, 0)),
            pl.BlockSpec((width, CZ), lambda g: (g, 0)),
            whole((size * size, CZ)),
            whole((CZ, size * size)),
            whole((1, CZ)),
            whole((levels, group * DEPTH_STEP, steps * size)),
            whole((steps * size, width)),
        ],
        out_specs=[
            pl.BlockSpec((width, CZ), lambda g: (g, 0)),
            pl.BlockSpec((1, size, group * seqs), lambda g: (g, 0, 0)),
            whole((seqs, size * width)),
            whole((size * size, CZ)),
        ],
        out_shape=[
            jax.ShapeDtypeStruct((steps * width, CZ), jnp.bfloat16),
            jax.ShapeDtypeStruct((steps, size, group * seqs), jnp.bfloat16),
            jax.ShapeDtypeStruct((seqs, size * width), jnp.float32),
            jax.ShapeDtypeStruct((size * size, CZ), jnp.float32),
        ],
        scratch_shapes=[
            pltpu.VMEM((size * size, width), jnp.bfloat16),
            pltpu.VMEM((steps * size, size * width), jnp.bfloat16),
            pltpu.VMEM((size * size, width), jnp.bfloat16),
        ],
        compiler_params=pltpu.CompilerParams(
            dimension_semantics=("arbitrary",), vmem_limit_bytes=56 * 1024 * 1024
        ),
    )(
        left_groups,
        right_wide,
        depth_rows,
        flat_grad,
        weight,
        weight.T,
        final_offset[None, :],
        left_levels,
        depth_tall,
    )
    pair_update = pair.reshape(rows, cols, CZ)
    left_sum = (
        left_grad.reshape(steps, size, group, seqs).transpose(3, 0, 2, 1).reshape(seqs, rows * size)
    )
    right_sum = (
        right_grad.reshape(seqs, size, group, cols)
        .sum(axis=2)
        .astype(jnp.bfloat16)
        .transpose(0, 2, 1)
        .reshape(seqs, cols * size)
    )
    adjoint_first_factor = lax.psum_scatter(left_sum, "col", scatter_dimension=0, tiled=True)
    right_parts = lax.all_to_all(right_sum, "col", split_axis=0, concat_axis=1, tiled=True)
    grad_right = lax.psum_scatter(right_parts, "row", scatter_dimension=1, tiled=True)
    weight_total = lax.psum(weight_part, ("row", "col"))
    grad_w_out = (
        weight_total.reshape(size, size, CZ).transpose(1, 0, 2).reshape(size * size, CZ)
        / WINDOW_AMINOS
    )
    return (pair_update, adjoint_first_factor, grad_right, grad_w_out)


def solution(mesh):
    in_specs = (
        P(("parts", "col"), "row", None),
        P(),
        P(),
        P(),
        P(),
        P(),
        P(),
        P("parts"),
        P("parts", None),
        P(("parts", "row"), "col", None),
    )
    out_specs = (
        P(("parts", "row"), "col", None),
        P(("parts", "col"), "row"),
        P(("parts", "col"), "row"),
        P("parts", None),
    )
    return jax.shard_map(shards, mesh=mesh, in_specs=in_specs, out_specs=out_specs, check_vma=False)
```

```python
import functools

import jax
import jax.numpy as jnp
from jax import lax
from jax.experimental import pallas as pl
from jax.experimental.pallas import tpu as pltpu
from jax.sharding import PartitionSpec as P

PROJECTED_SIZE = 32
CZ = 128
WINDOW_AMINOS = 256
DEPTH_STEP = 32
CHAINS = 8
LEVELS = 4


def standardize_entries(alignment_tensor, standard_multiplier, additive_offset):
    incoming_entries = alignment_tensor.astype(jnp.float32)
    center = incoming_entries - jnp.mean(incoming_entries, axis=-1, keepdims=True)
    spread = jnp.mean(center * center, axis=-1, keepdims=True)
    return (center * lax.rsqrt(spread + 1e-05) * standard_multiplier + additive_offset).astype(
        jnp.bfloat16
    )


def pair_kernel(
    group, cols, seqs, levels,
    left_ref, right_ref, depth_ref, grad_ref, weight_ref, weight_t_ref, bias_ref, left_t_ref,
    tall_ref,
    pair_ref, left_grad_ref, right_grad_ref, weight_grad_ref,
    outer_ref, scaled_ref, back_ref,
):
    step = pl.program_id(0)
    width = group * cols
    size = PROJECTED_SIZE
    chunk = 4
    depth = depth_ref[0]
    inverse = 1.0 / depth
    row = lax.broadcasted_iota(jnp.int32, (group * seqs, width), 0)
    lane = lax.broadcasted_iota(jnp.int32, (group * seqs, width), 1)
    seq = (row % seqs).astype(jnp.float32)
    keep = jnp.where(
        jnp.logical_and(row // seqs == lane // cols, seq < depth), 1.0, 0.0
    ).astype(jnp.bfloat16)
    keep = jnp.concatenate([keep] * chunk, axis=1)
    grad = grad_ref[...]
    back = lax.dot_general(
        weight_ref[...], grad, (((1,), (1,)), ((), ())), preferred_element_type=jnp.float32
    )
    back_ref[...] = (back * inverse).astype(jnp.bfloat16)
    left = left_ref[0]
    left_grad = jnp.zeros((size, group * seqs), jnp.float32)
    rows_here = pl.ds(pl.multiple_of(step * size, size), size)
    for first in range(0, size, chunk):
        lanes = slice(first * width, (first + chunk) * width)
        right = right_ref[:, lanes] * keep
        prod = jnp.dot(left, right, preferred_element_type=jnp.float32)
        for e in range(chunk):
            outer_ref[(first + e) * size : (first + e + 1) * size, :] = (
                prod[:, e * width : (e + 1) * width] * inverse
            ).astype(jnp.bfloat16)
        scaled = jnp.concatenate(
            [back_ref[(first + e) * size : (first + e + 1) * size, :] for e in range(chunk)], axis=1
        )
        scaled_ref[rows_here, lanes] = scaled
        left_grad = left_grad + lax.dot_general(
            scaled, right, (((1,), (1,)), ((), ())), preferred_element_type=jnp.float32
        )
    left_grad_ref[0] = left_grad.astype(jnp.bfloat16)
    outer = outer_ref[...]
    pair = jnp.dot(weight_t_ref[...], outer, preferred_element_type=jnp.float32).T
    pair_ref[...] = (pair + bias_ref[...]).astype(jnp.bfloat16)
    weight_part = jnp.dot(outer, grad, preferred_element_type=jnp.float32)

    @pl.when(step == 0)
    def _():
        weight_grad_ref[...] = weight_part

    @pl.when(step > 0)
    def _():
        weight_grad_ref[...] += weight_part

    @pl.when(step == pl.num_programs(0) - 1)
    def _():
        span = 2
        part = lax.broadcasted_iota(jnp.int32, (DEPTH_STEP, span * width), 1) % width // cols
        for level in range(levels):
            wanted = jnp.where(tall_ref[...] > level * DEPTH_STEP, 1.0, 0.0).astype(jnp.bfloat16)
            wanted = jnp.concatenate([wanted] * span, axis=1)

            def piece(index, carry, level=level, wanted=wanted):
                lanes = pl.ds(pl.multiple_of(index * span * width, span * width), span * width)
                masked = scaled_ref[:, lanes] * wanted
                out = jnp.dot(left_t_ref[level], masked, preferred_element_type=jnp.float32)
                total = jnp.zeros((DEPTH_STEP, span * width), jnp.float32)
                for g in range(group):
                    total = jnp.where(part == g, out[g * DEPTH_STEP : (g + 1) * DEPTH_STEP], total)
                right_grad_ref[level * DEPTH_STEP : (level + 1) * DEPTH_STEP, lanes] = total
                return carry

            lax.fori_loop(0, size // span, piece, 0)


def to(source, target, send, recv, row, col):
    return pltpu.make_async_remote_copy(
        src_ref=source,
        dst_ref=target,
        send_sem=send,
        recv_sem=recv,
        device_id={"row": row, "col": col},
        device_id_type=pl.DeviceIdType.MESH,
    )


def arrived(ref, sem):
    pltpu.make_async_copy(ref, ref, sem).wait()


def greet(n_row, n_col, me):
    peers = n_row * n_col
    barrier = pltpu.get_barrier_semaphore()

    def signal(off, carry):
        peer = (me + off) % peers
        pl.semaphore_signal(
            barrier,
            inc=1,
            device_id={"row": peer // n_col, "col": peer % n_col},
            device_id_type=pl.DeviceIdType.MESH,
        )
        return carry

    lax.fori_loop(1, peers, signal, 0)
    pl.semaphore_wait(barrier, peers - 1)


def sum_kernel(
    n_row, n_col, ratio,
    left_ref, right_ref, weight_ref,
    left_out, right_out, weight_out,
    left_in, right_in, weight_in, reduced, total,
    left_send, left_recv, right_send, right_recv,
    weight_send, weight_recv, total_send, total_recv,
):
    row, col = lax.axis_index("row"), lax.axis_index("col")
    me = row * n_col + col
    peers = n_row * n_col
    part = weight_ref.shape[0] // peers
    greet(n_row, n_col, me)

    def weight_copy(off):
        peer = (me + off) % peers
        source = weight_ref.at[pl.ds(pl.multiple_of(peer * part, part), part)]
        return to(
            source, weight_in.at[me], weight_send.at[off], weight_recv.at[me],
            peer // n_col, peer % n_col,
        )

    def total_copy(off):
        peer = (me + off) % peers
        return to(
            reduced, total.at[me], total_send.at[off], total_recv.at[me],
            peer // n_col, peer % n_col,
        )

    def left_copy(off):
        peer = (col + off) % n_col
        return to(
            left_ref.at[peer], left_in.at[col], left_send.at[off], left_recv.at[col], row, peer
        )

    owner = col // ratio
    slot = row * ratio + col % ratio

    def right_copy(off):
        peer = (col + off) % n_col
        return to(
            right_ref.at[peer], right_in.at[slot], right_send.at[off], right_recv.at[slot],
            owner, peer,
        )

    def start(make):
        def body(off, carry):
            make(off).start()
            return carry

        return body

    def sent(make):
        def body(off, carry):
            make(off).wait_send()
            return carry

        return body

    lax.fori_loop(1, peers, start(weight_copy), 0)
    lax.fori_loop(1, n_col, start(right_copy), 0)

    @pl.when(owner == row)
    def _():
        pltpu.make_async_copy(right_ref.at[col], right_in.at[slot], right_recv.at[slot]).start()

    @pl.when(owner != row)
    def _():
        right_copy(0).start()

    lax.fori_loop(1, n_col, start(left_copy), 0)

    def add_weight(off, acc):
        peer = (me + off) % peers
        arrived(weight_in.at[peer], weight_recv.at[peer])
        return acc + weight_in[peer]

    own = weight_ref[pl.ds(pl.multiple_of(me * part, part), part), :]
    mine = lax.fori_loop(1, peers, add_weight, own)
    reduced[...] = mine
    total[me] = mine
    lax.fori_loop(1, peers, sent(weight_copy), 0)
    lax.fori_loop(1, peers, start(total_copy), 0)

    def wait_left(off, carry):
        peer = (col + off) % n_col
        arrived(left_in.at[peer], left_recv.at[peer])
        return carry

    lax.fori_loop(1, n_col, wait_left, 0)
    left_total = left_ref[col].astype(jnp.float32)
    for off in range(1, n_col):
        left_total = left_total + left_in[(col + off) % n_col].astype(jnp.float32)
    left_out[...] = left_total.astype(jnp.bfloat16)
    width = right_in.shape[2]
    for t in range(ratio):
        right_total = jnp.zeros(right_in.shape[1:], jnp.float32)
        for r in range(n_row):
            arrived(right_in.at[r * ratio + t], right_recv.at[r * ratio + t])
            right_total = right_total + right_in[r * ratio + t].astype(jnp.float32)
        right_out[:, t * width : (t + 1) * width] = right_total.astype(jnp.bfloat16)

    def wait_total(off, carry):
        peer = (me + off) % peers
        arrived(total.at[peer], total_recv.at[peer])
        return carry

    lax.fori_loop(1, peers, wait_total, 0)
    weight_out[...] = total[...].reshape(weight_out.shape)
    lax.fori_loop(1, peers, sent(total_copy), 0)
    lax.fori_loop(1, n_col, sent(left_copy), 0)
    lax.fori_loop(1, n_col, sent(right_copy), 0)

    @pl.when(owner != row)
    def _():
        right_copy(0).wait_send()


def shards(
    alignment_tensor,
    standardizer_scaling,
    standardizer_offset,
    first_projector,
    second_projector,
    final_projector,
    final_offset,
    amino_strand_label,
    matched_strand_count,
    couple_delta_adjoint,
):
    homolog_portion, rows, embedding_extent = alignment_tensor.shape
    cols = couple_delta_adjoint.shape[1]
    size = PROJECTED_SIZE
    entries = standardize_entries(
        alignment_tensor, standardizer_scaling, standardizer_offset
    ).reshape(-1, embedding_extent)
    both = jnp.dot(
        entries,
        jnp.concatenate([first_projector, second_projector], axis=1),
        preferred_element_type=jnp.float32,
    ).astype(jnp.bfloat16)
    first_factor = both[:, :size].reshape(homolog_portion, rows * size)
    second_factor = both[:, size:].reshape(homolog_portion, rows * size)
    left_panel = lax.all_gather(first_factor, "col", axis=0, tiled=True)
    right_rows = lax.all_gather(second_factor, "row", axis=1, tiled=True)
    right_panel = lax.all_to_all(right_rows, "col", split_axis=1, concat_axis=0, tiled=True)
    seqs = left_panel.shape[0]
    levels = seqs // DEPTH_STEP
    row_start = lax.axis_index("row") * rows
    col_start = lax.axis_index("col") * cols
    chains = jnp.arange(CHAINS, dtype=jnp.int32)
    row_hot = (
        lax.dynamic_slice_in_dim(amino_strand_label, row_start, rows, 0)[:, None] == chains[None, :]
    ).astype(jnp.float32)
    col_hot = (
        lax.dynamic_slice_in_dim(amino_strand_label, col_start, cols, 0)[:, None] == chains[None, :]
    ).astype(jnp.float32)
    table = matched_strand_count.astype(jnp.float32)
    depth = jnp.dot(
        jnp.dot(row_hot, table, precision=lax.Precision.HIGHEST),
        col_hot.T,
        precision=lax.Precision.HIGHEST,
    )
    group = max(1, 128 // cols)
    width = group * cols
    steps = rows // group
    left4 = left_panel.reshape(seqs, steps, group, size)
    left_groups = left4.transpose(1, 3, 2, 0).reshape(steps, size, group * seqs)
    left_levels = (
        left_panel.reshape(levels, DEPTH_STEP, steps, group, size)
        .transpose(0, 3, 1, 2, 4)
        .reshape(levels, group * DEPTH_STEP, steps * size)
    )
    right_turned = right_panel.reshape(seqs, cols, size).transpose(0, 2, 1)
    right_wide = jnp.broadcast_to(
        right_turned[None, :, :, None, :], (group, seqs, size, group, cols)
    ).reshape(group * seqs, size * width)
    depth_rows = depth.reshape(steps, 1, width)
    depth_tall = jnp.broadcast_to(depth_rows, (steps, size, width)).reshape(steps * size, width)
    weight = final_projector.reshape(size, size, CZ).transpose(1, 0, 2).reshape(size * size, CZ)
    flat_grad = couple_delta_adjoint.reshape(-1, CZ)
    whole = lambda shape: pl.BlockSpec(shape, lambda g: (0,) * len(shape))
    pair, left_grad, right_grad, weight_part = pl.pallas_call(
        functools.partial(pair_kernel, group, cols, seqs, levels),
        grid=(steps,),
        in_specs=[
            pl.BlockSpec((1, size, group * seqs), lambda g: (g, 0, 0)),
            whole((group * seqs, size * width)),
            pl.BlockSpec((1, 1, width), lambda g: (g, 0, 0)),
            pl.BlockSpec((width, CZ), lambda g: (g, 0)),
            whole((size * size, CZ)),
            whole((CZ, size * size)),
            whole((1, CZ)),
            whole((levels, group * DEPTH_STEP, steps * size)),
            whole((steps * size, width)),
        ],
        out_specs=[
            pl.BlockSpec((width, CZ), lambda g: (g, 0)),
            pl.BlockSpec((1, size, group * seqs), lambda g: (g, 0, 0)),
            whole((seqs, size * width)),
            whole((size * size, CZ)),
        ],
        out_shape=[
            jax.ShapeDtypeStruct((steps * width, CZ), jnp.bfloat16),
            jax.ShapeDtypeStruct((steps, size, group * seqs), jnp.bfloat16),
            jax.ShapeDtypeStruct((seqs, size * width), jnp.float32),
            jax.ShapeDtypeStruct((size * size, CZ), jnp.float32),
        ],
        scratch_shapes=[
            pltpu.VMEM((size * size, width), jnp.bfloat16),
            pltpu.VMEM((steps * size, size * width), jnp.bfloat16),
            pltpu.VMEM((size * size, width), jnp.bfloat16),
        ],
        compiler_params=pltpu.CompilerParams(
            dimension_semantics=("arbitrary",), vmem_limit_bytes=56 * 1024 * 1024
        ),
    )(
        left_groups,
        right_wide,
        depth_rows,
        flat_grad,
        weight,
        weight.T,
        final_offset[None, :],
        left_levels,
        depth_tall,
    )
    pair_update = pair.reshape(rows, cols, CZ)
    left_sum = (
        left_grad.reshape(steps, size, group, seqs).transpose(3, 0, 2, 1).reshape(seqs, rows * size)
    )
    right_sum = (
        right_grad.reshape(seqs, size, group, cols)
        .sum(axis=2)
        .astype(jnp.bfloat16)
        .transpose(0, 2, 1)
        .reshape(seqs, cols * size)
    )
    n_row, n_col = lax.axis_size("row"), lax.axis_size("col")
    ratio = rows // cols
    peers = n_row * n_col
    vmem = pl.BlockSpec(memory_space=pltpu.VMEM)
    share = seqs // n_col
    part = weight_part.shape[0] // peers
    dma = pltpu.SemaphoreType.DMA
    adjoint_first_factor, grad_right, weight_total = pl.pallas_call(
        functools.partial(sum_kernel, n_row, n_col, ratio),
        in_specs=[vmem] * 3,
        out_specs=[vmem] * 3,
        out_shape=[
            jax.ShapeDtypeStruct((share, rows * size), jnp.bfloat16),
            jax.ShapeDtypeStruct((share, rows * size), jnp.bfloat16),
            jax.ShapeDtypeStruct(weight_part.shape, jnp.float32),
        ],
        scratch_shapes=[
            pltpu.VMEM((n_col, share, rows * size), jnp.bfloat16),
            pltpu.VMEM((n_row * ratio, share, cols * size), jnp.bfloat16),
            pltpu.VMEM((peers, part, CZ), jnp.float32),
            pltpu.VMEM((part, CZ), jnp.float32),
            pltpu.VMEM((peers, part, CZ), jnp.float32),
            dma((n_col,)),
            dma((n_col,)),
            dma((n_col,)),
            dma((n_row * ratio,)),
            dma((peers,)),
            dma((peers,)),
            dma((peers,)),
            dma((peers,)),
        ],
        compiler_params=pltpu.CompilerParams(collective_id=0, has_side_effects=True),
    )(
        left_sum.reshape(n_col, share, rows * size),
        right_sum.reshape(n_col, share, cols * size),
        weight_part,
    )
    grad_w_out = (
        weight_total.reshape(size, size, CZ).transpose(1, 0, 2).reshape(size * size, CZ)
        / WINDOW_AMINOS
    )
    return (pair_update, adjoint_first_factor, grad_right, grad_w_out)


def solution(mesh):
    in_specs = (
        P(("parts", "col"), "row", None),
        P(),
        P(),
        P(),
        P(),
        P(),
        P(),
        P("parts"),
        P("parts", None),
        P(("parts", "row"), "col", None),
    )
    out_specs = (
        P(("parts", "row"), "col", None),
        P(("parts", "col"), "row"),
        P(("parts", "col"), "row"),
        P("parts", None),
    )
    return jax.shard_map(shards, mesh=mesh, in_specs=in_specs, out_specs=out_specs, check_vma=False)
```
